32 devices in a mesh: hap: 2 (over x), snp: 16 (over z, y, core).
Axes of the slice: x: 2, y: 2, z: 4, core: 2. Of those that a mesh axis runs over, the one named last changes fastest.
Arguments:
- packed_panel: int32 [96, 16384], P('hap', 'snp'), may hold values from 0 to 8191, as said below
- components: bfloat16 [64, 1248], P(None, 'hap'), may hold values from -0.15625 to 0.15625
- bounds: int32 [2, 16384], P(None, 'snp'), may hold values from 0 to 16383, as said below
- band_width: int32 [16384], P('snp'), may hold values from 1 to 256
Outputs:
- ld_scores: float32 [16384], P('snp')
The draws below stay inside these ranges and needn't reach their ends.
Inputs may be any that keep to these rules, and one draw needn't show every extreme that they name: Bit j of packed_panel[w, s] (j from 0 to 12) is the allele of haplotype 13 w + j at SNP s; higher bits are zero. LD blocks are consecutive runs of 1 to 2048 SNPs that cover all SNPs in order; bounds[0, s] and bounds[1, s] are the first and last SNP of the block holding s.
All inputs are finite; a program needn't handle non-finite values.
Results may differ from the reference program's by a relative error of at most 0.00074.
Values may be sent and summed in bfloat16 or wider, within the bound.
No kernel may reach another device: no remote copies, remote signals or barrier semaphores. Data moves between devices by JAX's collectives and lax.ppermute only.
A program may use at most 64 MiB of HBM per device.

```python
import jax
import jax.numpy as jnp
from jax import lax

K = 64
SNP_DEV = 1024
HAPS = 1248
SNPS = 16384
BAND = 256
BLOCK_MOST = 2048
N_SNP = 16


def draw_packed_panel(key, part):
    positions = jnp.arange(SNPS, dtype=jnp.int32)
    trend = 100 + 600 * positions // SNPS
    jitter = jax.random.randint(jax.random.fold_in(key, 1), (SNPS,), -80, 81, dtype=jnp.int32)
    frequency = trend + jitter
    shifts = jnp.arange(13, dtype=jnp.int32)
    row_key = jax.random.fold_in(key, 2)

    def word_row(row_index):
        draws = jax.random.randint(jax.random.fold_in(row_key, row_index), (13, SNPS), 0, 1000, dtype=jnp.int32)
        bit_values = (draws < frequency[None, :]).astype(jnp.int32)
        return jnp.sum(jnp.left_shift(bit_values, shifts[:, None]), axis=0).astype(jnp.int32)
    return lax.map(word_row, jnp.arange(HAPS // 13, dtype=jnp.int32))


def draw_bounds(key, part):
    lengths = jax.random.randint(jax.random.fold_in(key, 3), (SNPS,), 2, BLOCK_MOST + 1, dtype=jnp.int32)
    single = jax.random.randint(jax.random.fold_in(key, 4), (SNPS,), 0, 8, dtype=jnp.int32)
    lengths = jnp.where(single == 0, 1, lengths)
    widest = jax.random.randint(jax.random.fold_in(key, 5), (), 0, 8, dtype=jnp.int32)
    positions = jnp.arange(SNPS, dtype=jnp.int32)
    lengths = jnp.where(positions == widest, BLOCK_MOST, lengths).astype(jnp.int32)
    block_ends = jnp.cumsum(lengths).astype(jnp.int32)
    block_index = jnp.searchsorted(block_ends, positions, side='right').astype(jnp.int32)
    block_first = block_ends[block_index] - lengths[block_index]
    block_last = jnp.minimum(block_ends[block_index] - 1, SNPS - 1)
    return jnp.stack([block_first, block_last]).astype(jnp.int32)


def place_ends(drawn, key, smallest, largest):
    place = [jax.random.randint(jax.random.fold_in(key, axis), (), 0, length) for axis, length in enumerate(drawn.shape)]
    main_axis = drawn.shape.index(max(drawn.shape))
    neighbour = place[:main_axis] + [(place[main_axis] + 1) % drawn.shape[main_axis]] + place[main_axis + 1:]
    return drawn.at[tuple(place)].set(smallest).at[tuple(neighbour)].set(largest)


def level_of(own_key, dims, pieces, least, largest):
    gain, own = 1.0, jax.random.fold_in(own_key, 6)
    for axis_at, parts in pieces:
        heights = jnp.exp(jax.random.uniform(jax.random.fold_in(own, axis_at), (parts,), jnp.float32, least / len(pieces), largest / len(pieces)))
        gain = gain * jnp.repeat(heights, dims[axis_at] // parts).reshape([-1 if axis == axis_at else 1 for axis in range(len(dims))])
    return gain


def scatter_about(rng, dims, deviation, reach, split=(), kind=jnp.bfloat16):
    values = jax.random.normal(rng, dims, jnp.float32) * deviation
    if len(split) > 0:
        values = level_of(rng, dims, split, -0.22, 0.18) * values
    return jnp.clip(values, min=-reach, max=reach).astype(kind)


def setup_inputs(seed: int = 0) -> dict:
    splits = jax.random.split(jax.random.key(seed), 5)
    packed_panel = draw_packed_panel(jax.random.fold_in(splits[4], 71), 0)
    components = scatter_about(splits[1], (K, HAPS), HAPS ** -0.5, 0.15625, ((1, 2),))
    bounds = draw_bounds(jax.random.fold_in(splits[4], 71), 0)
    band_width = place_ends(jax.random.randint(splits[3], (SNPS,), 1, BAND + 1), jax.random.fold_in(splits[3], 1), 1, BAND).astype(jnp.int32)
    return {"packed_panel": packed_panel, "components": components, "bounds": bounds, "band_width": band_width}


epsilon = 1e-06

def unpack(packed):
    shifts = jnp.arange(13, dtype=jnp.int32)
    bit_values = jnp.bitwise_and(jnp.right_shift(packed[:, None, :], shifts[None, :, None]), 1)
    return bit_values.reshape(packed.shape[0] * 13, packed.shape[1]).astype(jnp.bfloat16)

def standardize(factor):
    average = lax.optimization_barrier(jnp.mean(factor, axis=1, keepdims=True))
    centered = factor - average
    variance = lax.optimization_barrier(jnp.mean(centered * centered, axis=1, keepdims=True))
    return (centered * lax.rsqrt(variance + epsilon)).astype(jnp.bfloat16)

def band_scores(padded, inverse, bounds, band_width, offset, start_row, row_count, reach_width):
    component_count = padded.shape[0]
    block_size = min(256, row_count)

    def block_scores(block_index):
        first_row = start_row + block_index * block_size
        row_part = lax.dynamic_slice_in_dim(padded, first_row + reach_width, block_size, 1)
        column_part = lax.dynamic_slice_in_dim(padded, first_row, block_size + 2 * reach_width, 1)
        inverse_rows = lax.dynamic_slice_in_dim(inverse, first_row + reach_width, block_size, 0)
        inverse_columns = lax.dynamic_slice_in_dim(inverse, first_row, block_size + 2 * reach_width, 0)
        block_first = lax.dynamic_slice_in_dim(bounds[0], first_row, block_size, 0)
        block_last = lax.dynamic_slice_in_dim(bounds[1], first_row, block_size, 0)
        row_reach = lax.dynamic_slice_in_dim(band_width, first_row, block_size, 0)
        inner_products = lax.dot_general(row_part, column_part, (((0,), (0,)), ((), ())), preferred_element_type=jnp.float32)
        correlation = inner_products * (1.0 / component_count) * inverse_rows[:, None] * inverse_columns[None, :]
        row_position = offset + first_row + jnp.arange(block_size, dtype=jnp.int32)
        column_position = offset + first_row - reach_width + jnp.arange(block_size + 2 * reach_width, dtype=jnp.int32)
        window_low = jnp.maximum(block_first, row_position - row_reach)
        window_high = jnp.minimum(block_last, row_position + row_reach)
        inside = (column_position[None, :] >= window_low[:, None]) & (column_position[None, :] <= window_high[:, None]) & (column_position[None, :] != row_position[:, None])
        squared_sum = lax.optimization_barrier(jnp.sum(jnp.where(inside, correlation * correlation, 0.0), axis=1))
        window_count = lax.optimization_barrier(jnp.sum(inside.astype(jnp.float32), axis=1))
        return component_count * squared_sum / jnp.maximum(window_count, 1.0)
    blocks = jnp.arange(row_count // block_size, dtype=jnp.int32)
    return lax.map(block_scores, blocks).reshape(row_count)

def inverse_norms(padded):
    squares = jnp.square(padded.astype(jnp.float32))
    return lax.rsqrt(lax.optimization_barrier(jnp.mean(squares, axis=0)) + epsilon)

def reference(packed_panel, components, bounds, band_width):
    groups = packed_panel.reshape(packed_panel.shape[0], N_SNP, SNP_DEV).transpose(1, 0, 2)

    def project(packed):
        return jnp.dot(components, unpack(packed), preferred_element_type=jnp.float32)
    factor = lax.map(project, groups).transpose(1, 0, 2).reshape(components.shape[0], SNPS)
    normed = standardize(factor)
    padded = jnp.pad(normed, ((0, 0), (BAND, BAND)))
    inverse = inverse_norms(padded)
    return band_scores(padded, inverse, bounds, band_width, jnp.int32(0), 0, SNPS, BAND)
```

```python
import jax
import jax.numpy as jnp
from jax import lax
from jax.experimental import pallas as pl
from jax.experimental.pallas import tpu as pltpu
from jax.sharding import PartitionSpec as P

EPSILON = 1e-06
LANES = 128
SUBLANES = 8


def whole_in_vmem(count):
    return [pl.BlockSpec(memory_space=pltpu.VMEM)] * count


def project(components, packed_panel):
    rank, haps = components.shape
    words, columns = packed_panel.shape
    bits = haps // words

    def kernel(panel_ref, components_ref, out_ref, turned):
        turned[...] = components_ref[...].astype(jnp.float32).T
        weights = [turned[pl.ds(j, words, stride=bits), :] for j in range(bits)]
        weights = jnp.concatenate(weights, axis=0).astype(jnp.bfloat16)
        panel = panel_ref[...]
        alleles = [
            (jnp.right_shift(panel, j) & 1).astype(jnp.float32).astype(jnp.bfloat16)
            for j in range(bits)
        ]
        alleles = jnp.concatenate(alleles, axis=0)
        out_ref[...] = lax.dot_general(
            weights, alleles, (((0,), (0,)), ((), ())), preferred_element_type=jnp.float32
        )

    return pl.pallas_call(
        kernel,
        out_shape=jax.ShapeDtypeStruct((rank, columns), jnp.float32),
        in_specs=whole_in_vmem(2),
        out_specs=pl.BlockSpec(memory_space=pltpu.VMEM),
        scratch_shapes=[pltpu.VMEM((haps, rank), jnp.float32)],
        name="project",
    )(packed_panel, components)


def combine(own, other, reach):
    rank, columns = own.shape

    def kernel(own_ref, other_ref, factor_ref, near_ref, far_ref, moments_ref):
        odd = lax.rem(lax.axis_index("snp"), 2)
        factor = own_ref[...] + other_ref[...]
        factor_ref[...] = factor
        average = jnp.sum(factor, axis=1, keepdims=True) * (1.0 / columns)
        centered = factor - average
        deviation = jnp.sum(centered * centered, axis=1, keepdims=True)
        lane = lax.broadcasted_iota(jnp.int32, (rank, LANES), 1)
        moments_ref[...] = jnp.where(lane == 0, average, deviation).T[:SUBLANES]
        low = factor[:, :reach]
        high = factor[:, columns - reach :]
        near_ref[...] = jnp.where(odd == 1, low, high)
        far_ref[...] = jnp.where(odd == 1, high, low)

    edge = jax.ShapeDtypeStruct((rank, reach), jnp.float32)
    return pl.pallas_call(
        kernel,
        out_shape=(
            jax.ShapeDtypeStruct((rank, columns), jnp.float32),
            edge,
            edge,
            jax.ShapeDtypeStruct((SUBLANES, rank), jnp.float32),
        ),
        in_specs=whole_in_vmem(2),
        out_specs=tuple(whole_in_vmem(4)),
        name="combine",
    )(own, other)


def band_scores(factor, near, far, moments, bounds, band_width, total):
    rank, columns = factor.shape
    reach = near.shape[1]
    padded = columns + 2 * reach
    tile = LANES
    span = tile + 2 * reach

    def kernel(factor_ref, near_ref, far_ref, moments_ref, bounds_ref, width_ref, out_ref, turned, scale, normed_ref):
        place = lax.axis_index("snp")
        odd = lax.rem(place, 2)
        moments = jnp.concatenate([moments_ref[...]] * (LANES // rank), axis=1).T
        average = moments[:rank, 0:1]
        gain = lax.rsqrt(moments[:rank, 1:2] * (1.0 / total) + EPSILON)
        near, far = near_ref[...], far_ref[...]
        wide = jnp.concatenate(
            [jnp.where(odd == 1, near, far), factor_ref[...], jnp.where(odd == 1, far, near)], axis=1
        )
        normed = ((wide - average) * gain).astype(jnp.bfloat16)
        normed_ref[...] = normed
        exact = normed.astype(jnp.float32)
        squares = exact * exact
        inverse = lax.rsqrt(jnp.sum(squares, axis=0, keepdims=True) * (1.0 / rank) + EPSILON)
        turned[...] = exact.T.astype(jnp.bfloat16)
        upper = squares.astype(jnp.bfloat16)
        lower = (squares - upper.astype(jnp.float32)).astype(jnp.bfloat16)
        norms = lax.dot_general(
            jnp.concatenate([upper, lower], axis=0),
            jnp.ones((2 * rank, LANES), jnp.bfloat16),
            (((0,), (0,)), ((), ())),
            preferred_element_type=jnp.float32,
        )
        scale[...] = lax.rsqrt(norms * (1.0 / rank) + EPSILON)
        for first in range(0, columns, tile):
            position = first + lax.broadcasted_iota(jnp.int32, (1, tile), 1)
            width = width_ref[:, first : first + tile]
            start = bounds_ref[0:1, first : first + tile] - place * columns
            stop = bounds_ref[1:2, first : first + tile] - place * columns
            low = jnp.maximum(start, position - width)
            high = jnp.minimum(stop, position + width)
            low_in = low - (first - reach)
            high_in = high - (first - reach)
            rows = normed_ref[:, first + reach : first + reach + tile]
            products = jnp.dot(
                turned[first : first + span, :], rows, preferred_element_type=jnp.float32
            )
            products = products * scale[first : first + span, :]
            column = lax.broadcasted_iota(jnp.int32, (span, tile), 0)
            inside = (column >= low_in) & (column <= high_in)
            inside &= column != reach + lax.broadcasted_iota(jnp.int32, (span, tile), 1)
            summed = jnp.sum(jnp.where(inside, products * products, 0.0), axis=0, keepdims=True)
            own = inverse[:, first + reach : first + reach + tile]
            count = jnp.maximum(high - low, 1).astype(jnp.float32)
            out_ref[:, first : first + tile] = summed * (own * own) * (1.0 / rank) / count

    return pl.pallas_call(
        kernel,
        out_shape=jax.ShapeDtypeStruct((1, columns), jnp.float32),
        in_specs=whole_in_vmem(6),
        out_specs=pl.BlockSpec(memory_space=pltpu.VMEM),
        scratch_shapes=[
            pltpu.VMEM((padded, rank), jnp.bfloat16),
            pltpu.VMEM((padded, LANES), jnp.float32),
            pltpu.VMEM((rank, padded), jnp.bfloat16),
        ],
        name="band",
    )(factor, near, far, moments, bounds, band_width)


def swap(value, axis, distance):
    count = lax.axis_size(axis)
    return lax.ppermute(value, axis, [(i, i ^ distance) for i in range(count)])


def powers(count):
    steps = [1 << b for b in range(count.bit_length() - 1)]
    if 1 << len(steps) != count:
        raise ValueError("axis size")
    return steps


def on_device(packed_panel, components, bounds, band_width):
    columns = packed_panel.shape[1]
    reach = columns // 4
    devices = lax.axis_size("snp")
    partial = project(components, packed_panel)
    hap_steps = powers(lax.axis_size("hap"))
    for distance in hap_steps[:-1]:
        partial = partial + swap(partial, "hap", distance)
    other = swap(partial, "hap", hap_steps[-1])
    factor, near, far, moments = combine(partial, other, reach)
    outward = [(i, i + 1) for i in range(1, devices - 1, 2)]
    near = swap(near, "snp", 1)
    far = lax.ppermute(far, "snp", outward + [(j, i) for i, j in outward])
    row = lax.broadcasted_iota(jnp.int32, (SUBLANES, 1), 0)
    members = columns
    for distance in powers(devices):
        met = swap(moments, "snp", distance)
        gap = moments[0:1] - met[0:1]
        both = moments + met
        moments = jnp.where(row == 0, 0.5 * both, both + gap * gap * (0.5 * members))
        members *= 2
    scores = band_scores(factor, near, far, moments, bounds, band_width[None], members)
    return scores.reshape(columns)


def solution(mesh):
    in_specs = (P("hap", "snp"), P(None, "hap"), P(None, "snp"), P("snp"))
    return jax.shard_map(
        on_device, mesh=mesh, in_specs=in_specs, out_specs=P("snp"), check_vma=False
    )
```

```python
import jax
import jax.numpy as jnp
from jax import lax
from jax.experimental import pallas as pl
from jax.experimental.pallas import tpu as pltpu
from jax.sharding import PartitionSpec as P


EPSILON = 1e-06
LANES = 128
SUBLANES = 8
BLOCK = 256


def whole_in_vmem(count):
    return [pl.BlockSpec(memory_space=pltpu.VMEM)] * count


def project(components, packed_panel):
    rank, haps = components.shape
    words, columns = packed_panel.shape
    bits = haps // words

    def kernel(panel_ref, components_ref, out_ref, panel, weights_in, turned, arrived):
        copies = [
            pltpu.make_async_copy(components_ref, weights_in, arrived.at[0]),
            pltpu.make_async_copy(panel_ref, panel, arrived.at[1]),
        ]
        for copy in copies:
            copy.start()
        copies[0].wait()
        turned[...] = weights_in[...].astype(jnp.float32).T
        weights = [turned[pl.ds(j, words, stride=bits), :] for j in range(bits)]
        weights = jnp.concatenate(weights, axis=0).T.astype(jnp.bfloat16)
        copies[1].wait()
        step = min(BLOCK, columns)
        for first in range(0, columns, step):
            packed = panel[:, first : first + step]
            alleles = [
                (jnp.right_shift(packed, j) & 1).astype(jnp.float32).astype(jnp.bfloat16)
                for j in range(bits)
            ]
            out_ref[:, first : first + step] = jnp.dot(
                weights, jnp.concatenate(alleles, axis=0), preferred_element_type=jnp.float32
            )

    return pl.pallas_call(
        kernel,
        out_shape=jax.ShapeDtypeStruct((rank, columns), jnp.float32),
        in_specs=[pl.BlockSpec(memory_space=pltpu.HBM)] * 2,
        out_specs=pl.BlockSpec(memory_space=pltpu.VMEM),
        scratch_shapes=[
            pltpu.VMEM((words, columns), jnp.int32),
            pltpu.VMEM((rank, haps), jnp.bfloat16),
            pltpu.VMEM((haps, rank), jnp.float32),
            pltpu.SemaphoreType.DMA((2,)),
        ],
        compiler_params=pltpu.CompilerParams(vmem_limit_bytes=8 << 20),
        name="project",
    )(
        pltpu.with_memory_space_constraint(packed_panel, pltpu.HBM),
        pltpu.with_memory_space_constraint(components, pltpu.HBM),
    )


def windows(bounds, band_width):
    columns = bounds.shape[1]

    def kernel(bounds_ref, width_ref, low_ref, high_ref):
        offset = lax.axis_index("snp") * columns
        position = lax.broadcasted_iota(jnp.int32, (1, columns), 1)
        width = width_ref[...]
        low_ref[...] = jnp.maximum(bounds_ref[0:1] - offset, position - width)
        high_ref[...] = jnp.minimum(bounds_ref[1:2] - offset, position + width)

    edge = jax.ShapeDtypeStruct((1, columns), jnp.int32)
    return pl.pallas_call(
        kernel,
        out_shape=(edge, edge),
        in_specs=whole_in_vmem(2),
        out_specs=tuple(whole_in_vmem(2)),
        compiler_params=pltpu.CompilerParams(vmem_limit_bytes=2 << 20),
        name="windows",
    )(bounds, band_width)


def combine(own, other, reach):
    rank, columns = own.shape

    def kernel(own_ref, other_ref, factor_ref, near_ref, far_ref, moments_ref):
        odd = lax.rem(lax.axis_index("snp"), 2)
        factor = own_ref[...] + other_ref[...]
        factor_ref[...] = factor
        average = jnp.sum(factor, axis=1, keepdims=True) * (1.0 / columns)
        centered = factor - average
        deviation = jnp.sum(centered * centered, axis=1, keepdims=True)
        lane = lax.broadcasted_iota(jnp.int32, (rank, LANES), 1)
        moments_ref[...] = jnp.where(lane == 0, average, deviation).T[:SUBLANES]
        low = factor[:, :reach]
        high = factor[:, columns - reach :]
        near_ref[...] = jnp.where(odd == 1, low, high)
        far_ref[...] = jnp.where(odd == 1, high, low)

    edge = jax.ShapeDtypeStruct((rank, reach), jnp.float32)
    return pl.pallas_call(
        kernel,
        out_shape=(
            jax.ShapeDtypeStruct((rank, columns), jnp.float32),
            edge,
            edge,
            jax.ShapeDtypeStruct((SUBLANES, rank), jnp.float32),
        ),
        in_specs=whole_in_vmem(2),
        out_specs=tuple(whole_in_vmem(4)),
        compiler_params=pltpu.CompilerParams(vmem_limit_bytes=4 << 20),
        name="combine",
    )(own, other)


def band_scores(factor, near, far, moments, low, high, total):
    rank, columns = factor.shape
    reach = near.shape[1]
    padded = columns + 2 * reach
    tile = LANES
    span = tile + 2 * reach

    def kernel(factor_ref, near_ref, far_ref, moments_ref, low_ref, high_ref, out_ref, turned, scale, normed_ref):
        place = lax.axis_index("snp")
        odd = lax.rem(place, 2)
        moments = jnp.concatenate([moments_ref[...]] * (LANES // rank), axis=1).T
        average = moments[:rank, 0:1]
        gain = lax.rsqrt(moments[:rank, 1:2] * (1.0 / total) + EPSILON)
        near, far = near_ref[...], far_ref[...]
        wide = jnp.concatenate(
            [jnp.where(odd == 1, near, far), factor_ref[...], jnp.where(odd == 1, far, near)], axis=1
        )
        normed = ((wide - average) * gain).astype(jnp.bfloat16)
        normed_ref[...] = normed
        exact = normed.astype(jnp.float32)
        squares = exact * exact
        inverse = lax.rsqrt(jnp.sum(squares, axis=0, keepdims=True) * (1.0 / rank) + EPSILON)
        turned[...] = exact.T.astype(jnp.bfloat16)
        upper = squares.astype(jnp.bfloat16)
        lower = (squares - upper.astype(jnp.float32)).astype(jnp.bfloat16)
        norms = lax.dot_general(
            jnp.concatenate([upper, lower], axis=0),
            jnp.ones((2 * rank, LANES), jnp.bfloat16),
            (((0,), (0,)), ((), ())),
            preferred_element_type=jnp.float32,
        )
        scale[...] = lax.rsqrt(norms * (1.0 / rank) + EPSILON)
        for first in range(0, columns, tile):
            low = low_ref[:, first : first + tile]
            high = high_ref[:, first : first + tile]
            low_in = low - (first - reach)
            high_in = high - (first - reach)
            rows = normed_ref[:, first + reach : first + reach + tile]
            products = jnp.dot(
                turned[first : first + span, :], rows, preferred_element_type=jnp.float32
            )
            products = products * scale[first : first + span, :]
            column = lax.broadcasted_iota(jnp.int32, (span, tile), 0)
            inside = (column >= low_in) & (column <= high_in)
            inside &= column != reach + lax.broadcasted_iota(jnp.int32, (span, tile), 1)
            summed = jnp.sum(jnp.where(inside, products * products, 0.0), axis=0, keepdims=True)
            own = inverse[:, first + reach : first + reach + tile]
            count = jnp.maximum(high - low, 1).astype(jnp.float32)
            out_ref[:, first : first + tile] = summed * (own * own) * (1.0 / rank) / count

    return pl.pallas_call(
        kernel,
        out_shape=jax.ShapeDtypeStruct((1, columns), jnp.float32),
        in_specs=whole_in_vmem(6),
        out_specs=pl.BlockSpec(memory_space=pltpu.VMEM),
        scratch_shapes=[
            pltpu.VMEM((padded, rank), jnp.bfloat16),
            pltpu.VMEM((padded, LANES), jnp.float32),
            pltpu.VMEM((rank, padded), jnp.bfloat16),
        ],
        compiler_params=pltpu.CompilerParams(vmem_limit_bytes=8 << 20),
        name="band",
    )(factor, near, far, moments, low, high)


def swap(value, axis, distance):
    count = lax.axis_size(axis)
    return lax.ppermute(value, axis, [(i, i ^ distance) for i in range(count)])


def powers(count):
    steps = [1 << b for b in range(count.bit_length() - 1)]
    if 1 << len(steps) != count:
        raise ValueError("axis size")
    return steps


def merge(groups, members):
    row = lax.broadcasted_iota(jnp.int32, groups[0].shape, 0)
    total = sum(groups[1:], groups[0])
    average = total[0:1] * (1.0 / len(groups))
    gaps = [group[0:1] - average for group in groups]
    spread = sum([gap * gap for gap in gaps[1:]], gaps[0] * gaps[0])
    return jnp.where(row == 0, total * (1.0 / len(groups)), total + spread * float(members))


def on_device(packed_panel, components, bounds, band_width):
    columns = packed_panel.shape[1]
    reach = columns // 4
    devices = lax.axis_size("snp")
    partial = project(components, packed_panel)
    low, high = windows(bounds, band_width[None])
    hap_steps = powers(lax.axis_size("hap"))
    for distance in hap_steps[:-1]:
        partial = partial + swap(partial, "hap", distance)
    other = swap(partial, "hap", hap_steps[-1])
    factor, near, far, moments = combine(partial, other, reach)
    outward = [(i, i + 1) for i in range(1, devices - 1, 2)]
    near = swap(near, "snp", 1)
    far = lax.ppermute(far, "snp", outward + [(j, i) for i, j in outward])
    steps = powers(devices)
    rounds = [steps[:2]] + [[step] for step in steps[2:]]
    members = columns
    for round_steps in rounds:
        groups = [moments]
        for distance in range(round_steps[0], 2 * round_steps[-1], round_steps[0]):
            groups.append(swap(moments, "snp", distance))
        moments = merge(groups, members)
        members *= len(groups)
    scores = band_scores(factor, near, far, moments, low, high, members)
    return scores.reshape(columns)


def solution(mesh):
    in_specs = (P("hap", "snp"), P(None, "hap"), P(None, "snp"), P("snp"))
    return jax.shard_map(
        on_device, mesh=mesh, in_specs=in_specs, out_specs=P("snp"), check_vma=False
    )
```

```python
import jax
import jax.numpy as jnp
from jax import lax
from jax.experimental import pallas as pl
from jax.experimental.pallas import tpu as pltpu
from jax.sharding import PartitionSpec as P


EPSILON = 1e-06
LANES = 128
SUBLANES = 8
BLOCK = 256


def whole_in_vmem(count):
    return [pl.BlockSpec(memory_space=pltpu.VMEM)] * count


def split(value, upper_ref, lower_ref):
    rank, columns = value.shape
    center = jnp.sum(value, axis=1, keepdims=True) * (1.0 / columns)
    center = center.astype(jnp.bfloat16)
    rest = value - center.astype(jnp.float32)
    upper = rest.astype(jnp.bfloat16)
    upper_ref[:, :columns] = upper
    upper_ref[:, columns:] = jnp.broadcast_to(center, (rank, LANES))
    lower_ref[...] = (rest - upper.astype(jnp.float32)).astype(jnp.bfloat16)


def pieces(rank, columns):
    return (
        jax.ShapeDtypeStruct((rank, columns + LANES), jnp.bfloat16),
        jax.ShapeDtypeStruct((rank, columns), jnp.bfloat16),
    )


def split_sum(own, other):
    def kernel(own_ref, other_ref, upper_ref, lower_ref):
        split(own_ref[...] + other_ref[...], upper_ref, lower_ref)

    return pl.pallas_call(
        kernel,
        out_shape=pieces(*own.shape),
        in_specs=whole_in_vmem(2),
        out_specs=tuple(whole_in_vmem(2)),
        compiler_params=pltpu.CompilerParams(vmem_limit_bytes=4 << 20),
        name="split",
    )(own, other)


def project(components, packed_panel, in_pieces):
    rank, haps = components.shape
    words, columns = packed_panel.shape
    bits = haps // words

    def kernel(panel_ref, components_ref, *refs):
        outs, (panel, weights_in, turned, product, arrived) = refs[:-5], refs[-5:]
        copies = [
            pltpu.make_async_copy(components_ref, weights_in, arrived.at[0]),
            pltpu.make_async_copy(panel_ref, panel, arrived.at[1]),
        ]
        for copy in copies:
            copy.start()
        copies[0].wait()
        turned[...] = weights_in[...].astype(jnp.float32).T
        weights = [turned[pl.ds(j, words, stride=bits), :] for j in range(bits)]
        weights = jnp.concatenate(weights, axis=0).T.astype(jnp.bfloat16)
        copies[1].wait()
        step = min(BLOCK, columns)
        target = product if in_pieces else outs[0]
        for first in range(0, columns, step):
            packed = panel[:, first : first + step]
            alleles = [
                (jnp.right_shift(packed, j) & 1).astype(jnp.float32).astype(jnp.bfloat16)
                for j in range(bits)
            ]
            target[:, first : first + step] = jnp.dot(
                weights, jnp.concatenate(alleles, axis=0), preferred_element_type=jnp.float32
            )
        if in_pieces:
            split(product[...], *outs)

    whole = (jax.ShapeDtypeStruct((rank, columns), jnp.float32),)
    out_shape = pieces(rank, columns) if in_pieces else whole
    return pl.pallas_call(
        kernel,
        out_shape=out_shape,
        in_specs=[pl.BlockSpec(memory_space=pltpu.HBM)] * 2,
        out_specs=tuple(whole_in_vmem(len(out_shape))),
        scratch_shapes=[
            pltpu.VMEM((words, columns), jnp.int32),
            pltpu.VMEM((rank, haps), jnp.bfloat16),
            pltpu.VMEM((haps, rank), jnp.float32),
            pltpu.VMEM((rank, columns), jnp.float32),
            pltpu.SemaphoreType.DMA((2,)),
        ],
        compiler_params=pltpu.CompilerParams(vmem_limit_bytes=8 << 20),
        name="project",
    )(
        pltpu.with_memory_space_constraint(packed_panel, pltpu.HBM),
        pltpu.with_memory_space_constraint(components, pltpu.HBM),
    )


def windows(bounds, band_width):
    columns = bounds.shape[1]

    def kernel(bounds_ref, width_ref, low_ref, high_ref):
        offset = lax.axis_index("snp") * columns
        position = lax.broadcasted_iota(jnp.int32, (1, columns), 1)
        width = width_ref[...]
        low_ref[...] = jnp.maximum(bounds_ref[0:1] - offset, position - width)
        high_ref[...] = jnp.minimum(bounds_ref[1:2] - offset, position + width)

    edge = jax.ShapeDtypeStruct((1, columns), jnp.int32)
    return pl.pallas_call(
        kernel,
        out_shape=(edge, edge),
        in_specs=whole_in_vmem(2),
        out_specs=tuple(whole_in_vmem(2)),
        compiler_params=pltpu.CompilerParams(vmem_limit_bytes=2 << 20),
        name="windows",
    )(bounds, band_width)


def local_moments(upper, other_upper):
    rank, columns = upper.shape[0], upper.shape[1] - LANES

    def kernel(own_ref, other_ref, moments_ref):
        summed = own_ref[...].astype(jnp.float32) + other_ref[...].astype(jnp.float32)
        center = summed[:, columns:]
        factor = summed[:, :columns]
        average = jnp.sum(factor, axis=1, keepdims=True) * (1.0 / columns)
        centered = factor - average
        deviation = jnp.sum(centered * centered, axis=1, keepdims=True)
        lane = lax.broadcasted_iota(jnp.int32, (rank, LANES), 1)
        moments_ref[...] = jnp.where(lane == 0, average + center, deviation).T[:SUBLANES]

    return pl.pallas_call(
        kernel,
        out_shape=jax.ShapeDtypeStruct((SUBLANES, rank), jnp.float32),
        in_specs=whole_in_vmem(2),
        out_specs=pl.BlockSpec(memory_space=pltpu.VMEM),
        compiler_params=pltpu.CompilerParams(vmem_limit_bytes=4 << 20),
        name="local_moments",
    )(upper, other_upper)


def whole_factor(upper, other_upper, lower, other_lower, reach):
    rank, columns = lower.shape

    def kernel(upper_ref, other_upper_ref, lower_ref, other_lower_ref, factor_ref, near_ref, far_ref):
        odd = lax.rem(lax.axis_index("snp"), 2)
        high = upper_ref[...].astype(jnp.float32) + other_upper_ref[...].astype(jnp.float32)
        low = lower_ref[...].astype(jnp.float32) + other_lower_ref[...].astype(jnp.float32)
        factor = (high[:, :columns] + low) + high[:, columns : columns + 1]
        factor_ref[...] = factor
        first = factor[:, :reach]
        last = factor[:, columns - reach :]
        near_ref[...] = jnp.where(odd == 1, first, last)
        far_ref[...] = jnp.where(odd == 1, last, first)

    edge = jax.ShapeDtypeStruct((rank, reach), jnp.float32)
    return pl.pallas_call(
        kernel,
        out_shape=(jax.ShapeDtypeStruct((rank, columns), jnp.float32), edge, edge),
        in_specs=whole_in_vmem(4),
        out_specs=tuple(whole_in_vmem(3)),
        compiler_params=pltpu.CompilerParams(vmem_limit_bytes=4 << 20),
        name="whole_factor",
    )(upper, other_upper, lower, other_lower)


def band_scores(factor, near, far, moments, low, high, total):
    rank, columns = factor.shape
    reach = near.shape[1]
    padded = columns + 2 * reach
    tile = LANES
    span = tile + 2 * reach

    def kernel(factor_ref, near_ref, far_ref, moments_ref, low_ref, high_ref, out_ref, turned, scale, normed_ref):
        place = lax.axis_index("snp")
        odd = lax.rem(place, 2)
        moments = jnp.concatenate([moments_ref[...]] * (LANES // rank), axis=1).T
        average = moments[:rank, 0:1]
        gain = lax.rsqrt(moments[:rank, 1:2] * (1.0 / total) + EPSILON)
        near, far = near_ref[...], far_ref[...]
        wide = jnp.concatenate(
            [jnp.where(odd == 1, near, far), factor_ref[...], jnp.where(odd == 1, far, near)], axis=1
        )
        normed = ((wide - average) * gain).astype(jnp.bfloat16)
        normed_ref[...] = normed
        exact = normed.astype(jnp.float32)
        squares = exact * exact
        inverse = lax.rsqrt(jnp.sum(squares, axis=0, keepdims=True) * (1.0 / rank) + EPSILON)
        turned[...] = exact.T.astype(jnp.bfloat16)
        upper = squares.astype(jnp.bfloat16)
        lower = (squares - upper.astype(jnp.float32)).astype(jnp.bfloat16)
        norms = lax.dot_general(
            jnp.concatenate([upper, lower], axis=0),
            jnp.ones((2 * rank, LANES), jnp.bfloat16),
            (((0,), (0,)), ((), ())),
            preferred_element_type=jnp.float32,
        )
        scale[...] = lax.rsqrt(norms * (1.0 / rank) + EPSILON)
        for first in range(0, columns, tile):
            low = low_ref[:, first : first + tile]
            high = high_ref[:, first : first + tile]
            low_in = low - (first - reach)
            high_in = high - (first - reach)
            rows = normed_ref[:, first + reach : first + reach + tile]
            products = jnp.dot(
                turned[first : first + span, :], rows, preferred_element_type=jnp.float32
            )
            products = products * scale[first : first + span, :]
            column = lax.broadcasted_iota(jnp.int32, (span, tile), 0)
            inside = (column >= low_in) & (column <= high_in)
            inside &= column != reach + lax.broadcasted_iota(jnp.int32, (span, tile), 1)
            summed = jnp.sum(jnp.where(inside, products * products, 0.0), axis=0, keepdims=True)
            own = inverse[:, first + reach : first + reach + tile]
            count = jnp.maximum(high - low, 1).astype(jnp.float32)
            out_ref[:, first : first + tile] = summed * (own * own) * (1.0 / rank) / count

    return pl.pallas_call(
        kernel,
        out_shape=jax.ShapeDtypeStruct((1, columns), jnp.float32),
        in_specs=whole_in_vmem(6),
        out_specs=pl.BlockSpec(memory_space=pltpu.VMEM),
        scratch_shapes=[
            pltpu.VMEM((padded, rank), jnp.bfloat16),
            pltpu.VMEM((padded, LANES), jnp.float32),
            pltpu.VMEM((rank, padded), jnp.bfloat16),
        ],
        compiler_params=pltpu.CompilerParams(vmem_limit_bytes=8 << 20),
        name="band",
    )(factor, near, far, moments, low, high)


def swap(value, axis, distance):
    count = lax.axis_size(axis)
    return lax.ppermute(value, axis, [(i, i ^ distance) for i in range(count)])


def powers(count):
    steps = [1 << b for b in range(count.bit_length() - 1)]
    if 1 << len(steps) != count:
        raise ValueError("axis size")
    return steps


def merge(groups, members):
    row = lax.broadcasted_iota(jnp.int32, groups[0].shape, 0)
    total = sum(groups[1:], groups[0])
    average = total[0:1] * (1.0 / len(groups))
    gaps = [group[0:1] - average for group in groups]
    spread = sum([gap * gap for gap in gaps[1:]], gaps[0] * gaps[0])
    return jnp.where(row == 0, total * (1.0 / len(groups)), total + spread * float(members))


def on_device(packed_panel, components, bounds, band_width):
    columns = packed_panel.shape[1]
    reach = columns // 4
    devices = lax.axis_size("snp")
    hap_steps = powers(lax.axis_size("hap"))
    parts = project(components, packed_panel, len(hap_steps) == 1)
    low, high = windows(bounds, band_width[None])
    for distance in hap_steps[:-1]:
        other = swap(parts[0], "hap", distance)
        if distance == hap_steps[-2]:
            parts = split_sum(parts[0], other)
        else:
            parts = (parts[0] + other,)
    upper, lower = parts
    other_upper = swap(upper, "hap", hap_steps[-1])
    other_lower = swap(lower, "hap", hap_steps[-1])
    moments = local_moments(upper, other_upper)
    factor, near, far = whole_factor(upper, other_upper, lower, other_lower, reach)
    outward = [(i, i + 1) for i in range(1, devices - 1, 2)]
    near = swap(near, "snp", 1)
    far = lax.ppermute(far, "snp", outward + [(j, i) for i, j in outward])
    steps = powers(devices)
    rounds = [steps[:2]] + [[step] for step in steps[2:]]
    members = columns
    for round_steps in rounds:
        groups = [moments]
        for distance in range(round_steps[0], 2 * round_steps[-1], round_steps[0]):
            groups.append(swap(moments, "snp", distance))
        moments = merge(groups, members)
        members *= len(groups)
    scores = band_scores(factor, near, far, moments, low, high, members)
    return scores.reshape(columns)


def solution(mesh):
    in_specs = (P("hap", "snp"), P(None, "hap"), P(None, "snp"), P("snp"))
    return jax.shard_map(
        on_device, mesh=mesh, in_specs=in_specs, out_specs=P("snp"), check_vma=False
    )
```
